32 devices in a mesh: segment: 2 (over x), tok: 16 (over z, y, core).
Axes of the slice: x: 2, y: 2, z: 4, core: 2. Of those that a mesh axis runs over, the one named last changes fastest.
Arguments:
- inputs: bfloat16 [4096, 768], P('tok'), may hold values from -6 to 6
- keys: bfloat16 [2, 4096, 768], P('segment', 'tok'), may hold values from -6 to 6
- values: bfloat16 [2, 4096, 768], P('segment', 'tok'), may hold values from -8 to 8
- rates: float32 [2, 4096], P('segment', 'tok'), may hold values from 0.0002 to 0.003
- gains: float32 [2, 768], P('segment'), may hold values from 0.1 to 1.9
- w_in: bfloat16 [2, 384, 2, 768], P('segment', 'tok'), may hold values from -0.21875 to 0.21875
- w_out: bfloat16 [2, 768, 384], P('segment', 'tok'), may hold values from -0.3125 to 0.3125
Outputs:
- layer_outputs: bfloat16 [2, 4096, 768], P('segment', 'tok')
The draws below stay inside these ranges and needn't reach their ends.
All inputs are finite; a program needn't handle non-finite values.
Results may differ from the reference program's by a relative error of at most 0.028.
Values may be sent and summed in bfloat16 or wider, within the bound.
No kernel may reach another device: no remote copies, remote signals or barrier semaphores. Data moves between devices by JAX's collectives and lax.ppermute only.
A program may use at most 64 MiB of HBM per device.

```python
import math
import jax
import jax.numpy as jnp
from jax import lax

HD = 768
FH = 384
TOKENS = 4096
SEGMENTS = 2


def spiked(drawn, key, source, target, parts, factor):
    owner, partner = [(jnp.arange(drawn.shape[position]) // (drawn.shape[position] // parts)).reshape([-1 if axis == position else 1 for axis in range(drawn.ndim)]) for position in (source, target)]
    chosen = jax.random.permutation(key, parts)[partner]
    strong = (owner == chosen) | (owner == (partner + parts // 2) % parts)
    return jnp.where(strong, factor * drawn, drawn)


def shard_levels(stream_key, extent, shards, smallest, largest):
    def one(axis_at, parts):
        steps = jax.random.uniform(jax.random.fold_in(jax.random.fold_in(stream_key, 6), axis_at), (parts,), jnp.float32, smallest / len(shards), largest / len(shards))
        return jnp.repeat(jnp.exp(steps), extent[axis_at] // parts).reshape((-1,) + (1,) * (len(extent) - axis_at - 1))

    factor_of = one(*shards[0])
    for cut in shards[1:]:
        factor_of = factor_of * one(*cut)
    return factor_of


def noise(own_key, extent, width, most, cuts=(), held_as=jnp.bfloat16):
    loudness = shard_levels(own_key, extent, cuts, -0.22, 0.18) if cuts else 1.0
    result = jax.random.normal(own_key, extent, jnp.float32) * width * loudness
    return jnp.minimum(jnp.maximum(result, -most), most).astype(held_as)


def heavy_noise(stream_key, dims, scale, most, pieces, heavy, kind=jnp.bfloat16):
    drawn = scale * jax.random.normal(stream_key, dims, jnp.float32)
    if pieces:
        drawn = drawn * shard_levels(stream_key, dims, pieces, -0.22, 0.18)
    return jnp.clip(spiked(drawn, jax.random.fold_in(stream_key, 3), *heavy), -most, most).astype(kind)


def setup_inputs(seed: int = 0) -> dict:
    arg_keys = jax.random.split(jax.random.key(seed), 8)
    return {
        "inputs": noise(arg_keys[0], (TOKENS, HD), 1.0, 6.0, ((0, 16),)),
        "keys": noise(arg_keys[1], (SEGMENTS, TOKENS, HD), 1.0, 6.0, ((0, 2), (1, 16))),
        "values": heavy_noise(arg_keys[2], (SEGMENTS, TOKENS, HD), 1.0, 8.0, ((0, 2), (1, 16)), (1, 2, 16, 2.0)),
        "rates": jnp.clip(jnp.exp(math.log(0.003) - 2.7080502 * jax.random.uniform(arg_keys[3], (SEGMENTS, TOKENS), jnp.float32) ** shard_levels(arg_keys[3], (SEGMENTS, TOKENS), ((0, 2), (1, 16)), -0.2, 0.2)), 0.0002, 0.003),
        "gains": jnp.clip(1.0 + 0.18 * jax.random.normal(arg_keys[4], (SEGMENTS, HD), jnp.float32), 0.1, 1.9),
        "w_in": noise(arg_keys[5], (SEGMENTS, FH, 2, HD), HD ** -0.5, 0.21875, ((0, 2), (1, 16))),
        "w_out": noise(arg_keys[6], (SEGMENTS, HD, FH), FH ** -0.5, 0.3125, ((0, 2), (1, 16))),
    }


def renorm(weight, gradient):
    base = weight.astype(jnp.float32)
    moved = base + gradient
    base_rms = jnp.sqrt(lax.optimization_barrier(jnp.mean(base * base, axis=-1, keepdims=True)) + 1e-06)
    moved_rms = jnp.sqrt(lax.optimization_barrier(jnp.mean(moved * moved, axis=-1, keepdims=True)) + 1e-06)
    return (moved * (base_rms / moved_rms)).astype(jnp.bfloat16)

def apply_layer(rows_in, gain_row, fast_in, fast_out):
    rows32 = rows_in.astype(jnp.float32)
    scale = jax.lax.rsqrt(lax.optimization_barrier(jnp.mean(rows32 * rows32, axis=-1, keepdims=True)) + 1e-06)
    normed = (rows32 * scale * gain_row).astype(jnp.bfloat16)
    pre_act = jnp.einsum('td,fcd->tcf', normed.astype(jnp.float32), fast_in.astype(jnp.float32))
    gate_pre = pre_act[:, 0]
    mixed = (gate_pre * jax.nn.sigmoid(gate_pre) * pre_act[:, 1]).astype(jnp.bfloat16)
    branch = jnp.dot(mixed, fast_out.T, preferred_element_type=jnp.float32)
    return (rows32 + branch).astype(jnp.bfloat16)

def reference(inputs, keys, values, rates, gains, w_in, w_out):
    results = []
    current = inputs
    for layer_index in range(SEGMENTS):
        keys32 = keys[layer_index].astype(jnp.float32)
        hidden = jnp.einsum('td,fcd->tcf', keys32, w_in[layer_index].astype(jnp.float32))
        gate_pre = hidden[:, 0]
        up_pre = hidden[:, 1]
        sigmoid_h = jax.nn.sigmoid(gate_pre)
        silu_gate = gate_pre * sigmoid_h
        activation = (silu_gate * up_pre).astype(jnp.bfloat16)
        target = (rates[layer_index][:, None] * values[layer_index].astype(jnp.float32)).astype(jnp.bfloat16)
        d_act = jnp.dot(target, w_out[layer_index], preferred_element_type=jnp.float32)
        d_gate = d_act * up_pre * (sigmoid_h * (1.0 + gate_pre * (1.0 - sigmoid_h)))
        d_up = d_act * silu_gate
        d_hid = jnp.stack([d_gate, d_up], axis=1).astype(jnp.bfloat16)
        grad_in = jnp.einsum('tcf,td->fcd', d_hid.astype(jnp.float32), keys32)
        grad_out = jnp.dot(target.T, activation, preferred_element_type=jnp.float32)
        new_in = renorm(w_in[layer_index], grad_in)
        new_out = renorm(w_out[layer_index], grad_out)
        current = apply_layer(current, gains[layer_index], new_in, new_out)
        results.append(current)
    return jnp.stack(results)
```

```python
import jax
import jax.numpy as jnp
from jax import lax
from jax.sharding import PartitionSpec as P

EPS = 1e-06


def tok_shift(block, route):
    count = lax.axis_size("tok")
    return lax.ppermute(block, "tok", [(i, route(i)) for i in range(count)])


def pair_swap(block, mask):
    return tok_shift(block, lambda i: i ^ mask)


def outer_shift(block, distance, outer):
    return tok_shift(block, lambda i: ((i // 4 + distance) % outer) * 4 + i % 4)


def outer_gather(block, outer, place):
    pieces = jnp.zeros((outer,) + block.shape, block.dtype)
    for distance in range(outer):
        piece = outer_shift(block, distance, outer) if distance else block
        pieces = lax.dynamic_update_index_in_dim(pieces, piece, (place - distance) % outer, 0)
    return pieces


def outer_sum(pieces, outer, place):
    total = lax.dynamic_index_in_dim(pieces, place, 0, keepdims=False)
    for distance in range(1, outer):
        sent = lax.dynamic_index_in_dim(pieces, (place + distance) % outer, 0, keepdims=False)
        total = total + outer_shift(sent.astype(jnp.bfloat16), distance, outer).astype(jnp.float32)
    return total


def apply_layer(rows_in, gain_row, fast_gate, fast_up, fast_out, out_scale):
    rows32 = rows_in.astype(jnp.float32)
    scale = lax.rsqrt(jnp.mean(rows32 * rows32, axis=-1, keepdims=True) + EPS)
    normed = (rows32 * scale * gain_row).astype(jnp.bfloat16)
    gate_pre = jnp.einsum("td,fd->tf", normed, fast_gate, preferred_element_type=jnp.float32)
    up_pre = jnp.einsum("td,fd->tf", normed, fast_up, preferred_element_type=jnp.float32)
    mixed = (gate_pre * jax.nn.sigmoid(gate_pre) * up_pre).astype(jnp.bfloat16)
    branch = jnp.einsum("tf,jf->tj", mixed, fast_out, preferred_element_type=jnp.float32)
    return (rows32 + branch * out_scale).astype(jnp.bfloat16)


def per_device(inputs, keys, values, rates, gains, w_in, w_out):
    own_keys = keys[0]
    own_target = (rates[0][:, None] * values[0].astype(jnp.float32)).astype(jnp.bfloat16)
    width = own_keys.shape[1]
    outer = lax.axis_size("tok") // 4
    index = lax.axis_index("tok")
    place, corner = index // 4, index % 4
    f_rows, j_rows = w_in.shape[1], w_out.shape[1]
    quarter = outer * f_rows

    y_keys, y_target = pair_swap(own_keys, 2), pair_swap(own_target, 2)
    all_keys = jnp.concatenate([own_keys, pair_swap(own_keys, 1), y_keys, pair_swap(y_keys, 1)], 0)
    all_target = jnp.concatenate([own_target, pair_swap(own_target, 1), y_target, pair_swap(y_target, 1)], 0)

    own_in = w_in[0].transpose(1, 0, 2)
    by_corner = w_out[0].reshape(j_rows, outer, 4, f_rows).transpose(2, 0, 1, 3).reshape(4, j_rows, quarter)
    slab = jnp.zeros((4, j_rows, quarter), jnp.bfloat16)
    for mask in range(4):
        piece = lax.dynamic_index_in_dim(by_corner, corner ^ mask, 0, keepdims=False)
        piece = pair_swap(piece, mask) if mask else piece
        slab = lax.dynamic_update_index_in_dim(slab, piece, corner ^ mask, 0)
    slab = slab.reshape(4 * j_rows, quarter)
    whole_in = outer_gather(own_in, outer, place).transpose(1, 0, 2, 3).reshape(2, quarter, width)
    whole_out = outer_gather(slab, outer, place).reshape(outer * 4 * j_rows, quarter)

    base_part = jnp.sum(jnp.square(whole_out.astype(jnp.float32)), axis=-1)
    base_part = base_part + pair_swap(base_part, 1)
    base_sum = base_part + pair_swap(base_part, 2)

    gate_pre = jnp.einsum("td,fd->tf", all_keys, whole_in[0], preferred_element_type=jnp.float32)
    up_pre = jnp.einsum("td,fd->tf", all_keys, whole_in[1], preferred_element_type=jnp.float32)
    d_act = jnp.dot(all_target, whole_out, preferred_element_type=jnp.float32)
    sigmoid_h = jax.nn.sigmoid(gate_pre)
    silu_gate = gate_pre * sigmoid_h
    activation = (silu_gate * up_pre).astype(jnp.bfloat16)
    d_gate = (d_act * up_pre * (sigmoid_h * (1.0 + gate_pre * (1.0 - sigmoid_h)))).astype(jnp.bfloat16)
    d_up = (d_act * silu_gate).astype(jnp.bfloat16)
    g_gate = jnp.einsum("tf,td->fd", d_gate, all_keys, preferred_element_type=jnp.float32)
    g_up = jnp.einsum("tf,td->fd", d_up, all_keys, preferred_element_type=jnp.float32)
    g_out = jnp.einsum("tj,tf->jf", all_target, activation, preferred_element_type=jnp.float32)

    g_in = jnp.stack([g_gate.reshape(outer, f_rows, width), g_up.reshape(outer, f_rows, width)], 1)
    grad_in = outer_sum(g_in, outer, place)
    grad_out = outer_sum(g_out.reshape(outer, 4 * j_rows, quarter), outer, place)

    base = own_in.astype(jnp.float32)
    moved = base + grad_in
    base_rms = jnp.sqrt(jnp.mean(base * base, axis=-1, keepdims=True) + EPS)
    moved_rms = jnp.sqrt(jnp.mean(moved * moved, axis=-1, keepdims=True) + EPS)
    new_in = (moved * (base_rms / moved_rms)).astype(jnp.bfloat16)
    moved_out = (slab.astype(jnp.float32) + grad_out).astype(jnp.bfloat16)

    fast_in = outer_gather(new_in, outer, place).transpose(1, 0, 2, 3).reshape(2, quarter, width)
    fast_out = outer_gather(moved_out, outer, place).reshape(outer * 4 * j_rows, quarter)
    for mask in (2, 1):
        fast_in = jnp.concatenate([fast_in, pair_swap(fast_in, mask)], 1)
        fast_out = jnp.concatenate([fast_out, pair_swap(fast_out, mask)], 1)
    units = fast_out.shape[1]
    moved_sum = jnp.sum(jnp.square(fast_out.astype(jnp.float32)), axis=-1)
    out_scale = (jnp.sqrt(base_sum / units + EPS) / jnp.sqrt(moved_sum / units + EPS))[None, :]

    depth = lax.axis_size("segment")
    first = lax.axis_index("segment") == 0
    finished = apply_layer(inputs, gains[0], fast_in[0], fast_in[1], fast_out, out_scale)
    for _ in range(depth - 1):
        arrived = lax.ppermute(finished, "segment", [(i, i + 1) for i in range(depth - 1)])
        current = jnp.where(first, inputs, arrived)
        finished = apply_layer(current, gains[0], fast_in[0], fast_in[1], fast_out, out_scale)
    return finished[None]


def solution(mesh):
    in_specs = (
        P("tok", None),
        P("segment", "tok", None),
        P("segment", "tok", None),
        P("segment", "tok"),
        P("segment", None),
        P("segment", "tok", None, None),
        P("segment", "tok", None),
    )
    out_specs = P("segment", "tok", None)
    return jax.shard_map(
        per_device, mesh=mesh, in_specs=in_specs, out_specs=out_specs, check_vma=False
    )
```

```python
import functools

import jax
import jax.numpy as jnp
import numpy as np
from jax import lax
from jax.experimental import pallas as pl
from jax.experimental.pallas import tpu as pltpu
from jax.sharding import PartitionSpec as P

EPS = 1e-06
LANES = 128
F32, BF16 = jnp.float32, jnp.bfloat16


def tok_shift(block, route):
    count = lax.axis_size("tok")
    return lax.ppermute(block, "tok", [(i, route(i)) for i in range(count)])


def pair_swap(block, mask):
    return tok_shift(block, lambda i: i ^ mask)


def outer_shift(block, distance, outer):
    return tok_shift(block, lambda i: ((i // 4 + distance) % outer) * 4 + i % 4)


def call(body, name, outs, *args, scratch=(), flops=0):
    moved = sum(a.size * a.dtype.itemsize for a in args) + sum(o.size * o.dtype.itemsize for o in outs)
    return pl.pallas_call(
        body,
        name=name,
        out_shape=tuple(outs),
        in_specs=[pl.BlockSpec(memory_space=pltpu.VMEM)] * len(args),
        out_specs=tuple(pl.BlockSpec(memory_space=pltpu.VMEM) for _ in outs),
        scratch_shapes=list(scratch),
        cost_estimate=pl.CostEstimate(flops=flops, bytes_accessed=moved, transcendentals=0),
    )(*args)


def like(shape, dtype=BF16):
    return jax.ShapeDtypeStruct(shape, dtype)


def dot_nt(a, b):
    return lax.dot_general(a, b, (((1,), (1,)), ((), ())), preferred_element_type=F32)


def dot_nn(a, b):
    return lax.dot_general(a, b, (((1,), (0,)), ((), ())), preferred_element_type=F32)


def pack(block):
    rows, cols = block.shape
    whole = cols // LANES * LANES
    parts = [block[:, i : i + LANES] for i in range(0, whole, LANES)]
    if cols > whole:
        ways = LANES // (cols - whole)
        step = rows // ways
        parts.append(jnp.concatenate([block[i * step : (i + 1) * step, whole:] for i in range(ways)], 1))
    return jnp.concatenate(parts, 0)


def unpack(packed, rows, cols):
    whole = cols // LANES * LANES
    parts = [packed[i * rows : (i + 1) * rows] for i in range(whole // LANES)]
    if cols > whole:
        rest = cols - whole
        tail = packed[whole // LANES * rows :]
        parts.append(jnp.concatenate([tail[:, i : i + rest] for i in range(0, LANES, rest)], 0))
    return jnp.concatenate(parts, 1)


def prepare_body(values, rates, w_in, w_out, order, target, own_in, *rest):
    pieces, by_corner = rest[:4], rest[4]
    corner = lax.axis_index("tok") % 4
    wide = jnp.broadcast_to(rates[...], (8, rates.shape[1]))
    column = wide.T[:, 0:1]
    target[...] = (column * values[...].astype(F32)).astype(BF16)
    pair = w_in[...].astype(F32)
    own_in[0] = pair[:, 0, :].astype(BF16)
    own_in[1] = pair[:, 1, :].astype(BF16)
    sorted_out = dot_nn(w_out[...], order[...])
    quarter = by_corner.shape[2]
    for c in range(4):
        by_corner[c] = sorted_out[:, c * quarter : (c + 1) * quarter]
    for mask in range(4):
        pieces[mask][...] = by_corner[corner ^ mask].astype(BF16)


def slab_body(*refs):
    pieces, slab, rows = refs[:4], refs[4], refs[5]
    corner = lax.axis_index("tok") % 4
    for mask in range(4):
        rows[corner ^ mask] = pieces[mask][...].astype(F32)
    block = rows[...]
    slab[...] = pack(block.reshape(block.shape[0] * block.shape[1], block.shape[2]).T).astype(BF16)


def place_in(pieces, out, outer):
    place = lax.axis_index("tok") // 4
    for k in range(outer):
        home = lax.rem(place + outer - k, outer)
        out[0, home] = pieces[k][0]
        out[1, home] = pieces[k][1]


def place_out(pieces, spread, outer, rows, cols):
    place = lax.axis_index("tok") // 4
    for k in range(outer):
        spread[lax.rem(place + outer - k, outer)] = pieces[k][...].astype(F32)
    return jnp.concatenate([unpack(spread[z], rows, cols) for z in range(outer)], 1)


def grads(keys, target, w_gate, w_up, w_down):
    gate_pre, up_pre = dot_nt(w_gate, keys), dot_nt(w_up, keys)
    d_act = dot_nt(w_down, target)
    sigmoid_h = jax.nn.sigmoid(gate_pre)
    silu_gate = gate_pre * sigmoid_h
    activation = (silu_gate * up_pre).astype(BF16)
    d_gate = (d_act * up_pre * (sigmoid_h * (1.0 + gate_pre * (1.0 - sigmoid_h)))).astype(BF16)
    d_up = (d_act * silu_gate).astype(BF16)
    return dot_nn(d_gate, keys), dot_nn(d_up, keys), dot_nn(activation, target)


def rows_of(ref, index):
    block = ref[index].astype(F32)
    return block.reshape(block.shape[0] * block.shape[1], block.shape[2]).astype(BF16)


def near_body(outer, cols, *refs):
    in_pieces, out_pieces = refs[:outer], refs[outer : 2 * outer]
    keys_a, keys_b, target_a, target_b = refs[2 * outer : 2 * outer + 4]
    whole_in, whole_out, base_part, acc_gate, acc_up, acc_out = refs[2 * outer + 4 : 2 * outer + 10]
    spread = refs[2 * outer + 10]
    place_in(in_pieces, whole_in, outer)
    w_down = place_out(out_pieces, spread, outer, acc_gate.shape[0], cols)
    base_part[...] = jnp.sum(w_down * w_down, axis=0, keepdims=True)
    w_down = w_down.astype(BF16)
    whole_out[...] = w_down
    w_gate, w_up = rows_of(whole_in, 0), rows_of(whole_in, 1)
    first = grads(keys_a[...], target_a[...], w_gate, w_up, w_down)
    second = grads(keys_b[...], target_b[...], w_gate, w_up, w_down)
    for ref, a, b in zip((acc_gate, acc_up, acc_out), first, second):
        ref[...] = a + b


def far_body(outer, cols, *refs):
    whole_in, whole_out, keys_a, keys_b, target_a, target_b, acc_gate, acc_up, acc_out = refs[:9]
    in_sent, out_sent = refs[9 : 9 + outer], refs[9 + outer : 9 + 2 * outer]
    spread_gate, spread_up, spread_out = refs[9 + 2 * outer :]
    place = lax.axis_index("tok") // 4
    w_gate, w_up, w_down = rows_of(whole_in, 0), rows_of(whole_in, 1), whole_out[...]
    first = grads(keys_a[...], target_a[...], w_gate, w_up, w_down)
    second = grads(keys_b[...], target_b[...], w_gate, w_up, w_down)
    total = [ref[...] + a + b for ref, a, b in zip((acc_gate, acc_up, acc_out), first, second)]
    spread_gate[...] = total[0].reshape(spread_gate.shape)
    spread_up[...] = total[1].reshape(spread_up.shape)
    for z in range(outer):
        spread_out[z] = pack(total[2][:, z * cols : (z + 1) * cols])
    for k in range(outer):
        home = lax.rem(place + k, outer)
        in_sent[k][0] = spread_gate[home].astype(in_sent[k].dtype)
        in_sent[k][1] = spread_up[home].astype(in_sent[k].dtype)
        out_sent[k][...] = spread_out[home].astype(out_sent[k].dtype)


def join_in_body(outer, *refs):
    place_in(refs[:outer], refs[outer], outer)


def join_out_body(outer, cols, *refs):
    whole, spread = refs[outer], refs[outer + 1]
    whole[...] = place_out(refs[:outer], spread, outer, whole.shape[0], cols).astype(BF16)


def layer_body(rows_a, rows_b, gain, base_sum, *refs):
    in_parts, out_parts, result = refs[:4], refs[4:8], refs[8]
    rows = jnp.where(lax.axis_index("segment") == 0, rows_a[...], rows_b[...])
    rows32 = rows.astype(F32)
    scale = lax.rsqrt(jnp.mean(rows32 * rows32, axis=-1, keepdims=True) + EPS)
    normed = (rows32 * scale * gain[...]).astype(BF16)
    w_gate = jnp.concatenate([part[0] for part in in_parts], 0)
    w_up = jnp.concatenate([part[1] for part in in_parts], 0)
    w_down = jnp.concatenate([part[...] for part in out_parts], 0)
    units = w_down.shape[0]
    wide = w_down.astype(F32)
    moved_sum = jnp.sum(wide * wide, axis=0, keepdims=True)
    out_scale = jnp.sqrt(base_sum[...] / units + EPS) / jnp.sqrt(moved_sum / units + EPS)
    gate_pre, up_pre = dot_nt(normed, w_gate), dot_nt(normed, w_up)
    mixed = (gate_pre * jax.nn.sigmoid(gate_pre) * up_pre).astype(BF16)
    result[...] = (rows32 + dot_nn(mixed, w_down) * out_scale).astype(BF16)


def column_order(outer, f_rows):
    units = outer * 4 * f_rows
    source = np.arange(units).reshape(outer, 4, f_rows).transpose(1, 0, 2).reshape(-1)
    order = np.zeros((units, units), np.float32)
    order[source, np.arange(units)] = 1.0
    return jnp.asarray(order, BF16)


def fast_device(inputs, keys, values, rates, gains, w_in, w_out):
    own_keys = keys[0]
    tokens, width = own_keys.shape
    outer = lax.axis_size("tok") // 4
    f_rows, j_rows = w_in.shape[1], w_out.shape[1]
    quarter, cols = outer * f_rows, 4 * j_rows
    packed = (quarter * cols // LANES, LANES)

    y_keys = pair_swap(own_keys, 2)
    made = call(
        prepare_body,
        "prepare",
        [like((tokens, width)), like((2, f_rows, width))] + [like((j_rows, quarter))] * 4,
        values[0], rates, w_in[0], w_out[0], column_order(outer, f_rows),
        scratch=[pltpu.VMEM((4, j_rows, quarter), F32)],
    )
    own_target, own_in, pieces = made[0], made[1], made[2:]
    pieces = [pieces[0]] + [pair_swap(pieces[mask], mask) for mask in (1, 2, 3)]
    (slab,) = call(
        slab_body, "slab", [like(packed)], *pieces, scratch=[pltpu.VMEM((4, j_rows, quarter), F32)]
    )
    in_pieces = [own_in] + [outer_shift(own_in, k, outer) for k in range(1, outer)]
    y_target = pair_swap(own_target, 2)
    core_keys, core_target = pair_swap(own_keys, 1), pair_swap(own_target, 1)
    far_keys, far_target = pair_swap(y_keys, 1), pair_swap(y_target, 1)
    out_pieces = [slab] + [outer_shift(slab, k, outer) for k in range(1, outer)]

    spread = pltpu.VMEM((outer,) + packed, F32)
    work = 2 * 2 * 6 * tokens * width * quarter
    whole_in, whole_out, base_part, acc_gate, acc_up, acc_out = call(
        functools.partial(near_body, outer, cols),
        "near",
        [like((2, outer, f_rows, width)), like((quarter, width)), like((1, width), F32)]
        + [like((quarter, width), F32)] * 3,
        *in_pieces, *out_pieces, own_keys, core_keys, own_target, core_target,
        scratch=[spread],
        flops=work,
    )
    base_part = base_part + pair_swap(base_part, 1)
    base_sum = base_part + pair_swap(base_part, 2)
    made = call(
        functools.partial(far_body, outer, cols),
        "far",
        [like((2, f_rows, width), BF16 if k else F32) for k in range(outer)]
        + [like(packed, BF16 if k else F32) for k in range(outer)],
        whole_in, whole_out, y_keys, far_keys, y_target, far_target, acc_gate, acc_up, acc_out,
        scratch=[pltpu.VMEM((outer, f_rows, width), F32)] * 2 + [spread],
        flops=work,
    )
    grad_in, grad_out = made[0], made[outer]
    for k in range(1, outer):
        grad_in = grad_in + outer_shift(made[k], k, outer).astype(F32)
    for k in range(1, outer):
        grad_out = grad_out + outer_shift(made[outer + k], k, outer).astype(F32)

    base = own_in.astype(F32)
    moved = base + grad_in
    base_rms = jnp.sqrt(jnp.mean(base * base, axis=-1, keepdims=True) + EPS)
    moved_rms = jnp.sqrt(jnp.mean(moved * moved, axis=-1, keepdims=True) + EPS)
    new_in = (moved * (base_rms / moved_rms)).astype(BF16)
    moved_out = (slab.astype(F32) + grad_out).astype(BF16)

    (fast_in,) = call(
        functools.partial(join_in_body, outer),
        "join_in",
        [like((2, outer, f_rows, width))],
        new_in, *[outer_shift(new_in, k, outer) for k in range(1, outer)],
    )
    fast_in = fast_in.reshape(2, quarter, width)
    (fast_out,) = call(
        functools.partial(join_out_body, outer, cols),
        "join_out",
        [like((quarter, width))],
        moved_out, *[outer_shift(moved_out, k, outer) for k in range(1, outer)],
        scratch=[spread],
    )
    weights = []
    for own in (fast_in, fast_out):
        other = pair_swap(own, 2)
        weights += [own, other, pair_swap(own, 1), pair_swap(other, 1)]

    def apply_layer(arrived):
        (rows,) = call(
            layer_body, "layer", [like(inputs.shape)], inputs, arrived, gains, base_sum, *weights,
            flops=6 * tokens * width * 4 * quarter,
        )
        return rows

    depth = lax.axis_size("segment")
    finished = apply_layer(inputs)
    for _ in range(depth - 1):
        finished = apply_layer(lax.ppermute(finished, "segment", [(i, i + 1) for i in range(depth - 1)]))
    return finished[None]


def outer_gather(block, outer, place):
    pieces = jnp.zeros((outer,) + block.shape, block.dtype)
    for distance in range(outer):
        piece = outer_shift(block, distance, outer) if distance else block
        pieces = lax.dynamic_update_index_in_dim(pieces, piece, (place - distance) % outer, 0)
    return pieces


def outer_sum(pieces, outer, place):
    total = lax.dynamic_index_in_dim(pieces, place, 0, keepdims=False)
    for distance in range(1, outer):
        sent = lax.dynamic_index_in_dim(pieces, (place + distance) % outer, 0, keepdims=False)
        total = total + outer_shift(sent.astype(jnp.bfloat16), distance, outer).astype(jnp.float32)
    return total


def apply_layer(rows_in, gain_row, fast_gate, fast_up, fast_out, out_scale):
    rows32 = rows_in.astype(jnp.float32)
    scale = lax.rsqrt(jnp.mean(rows32 * rows32, axis=-1, keepdims=True) + EPS)
    normed = (rows32 * scale * gain_row).astype(jnp.bfloat16)
    gate_pre = jnp.einsum("td,fd->tf", normed, fast_gate, preferred_element_type=jnp.float32)
    up_pre = jnp.einsum("td,fd->tf", normed, fast_up, preferred_element_type=jnp.float32)
    mixed = (gate_pre * jax.nn.sigmoid(gate_pre) * up_pre).astype(jnp.bfloat16)
    branch = jnp.einsum("tf,jf->tj", mixed, fast_out, preferred_element_type=jnp.float32)
    return (rows32 + branch * out_scale).astype(jnp.bfloat16)


def plain_device(inputs, keys, values, rates, gains, w_in, w_out):
    own_keys = keys[0]
    own_target = (rates[0][:, None] * values[0].astype(jnp.float32)).astype(jnp.bfloat16)
    width = own_keys.shape[1]
    outer = lax.axis_size("tok") // 4
    index = lax.axis_index("tok")
    place, corner = index // 4, index % 4
    f_rows, j_rows = w_in.shape[1], w_out.shape[1]
    quarter = outer * f_rows

    y_keys, y_target = pair_swap(own_keys, 2), pair_swap(own_target, 2)
    all_keys = jnp.concatenate([own_keys, pair_swap(own_keys, 1), y_keys, pair_swap(y_keys, 1)], 0)
    all_target = jnp.concatenate([own_target, pair_swap(own_target, 1), y_target, pair_swap(y_target, 1)], 0)

    own_in = w_in[0].transpose(1, 0, 2)
    by_corner = w_out[0].reshape(j_rows, outer, 4, f_rows).transpose(2, 0, 1, 3).reshape(4, j_rows, quarter)
    slab = jnp.zeros((4, j_rows, quarter), jnp.bfloat16)
    for mask in range(4):
        piece = lax.dynamic_index_in_dim(by_corner, corner ^ mask, 0, keepdims=False)
        piece = pair_swap(piece, mask) if mask else piece
        slab = lax.dynamic_update_index_in_dim(slab, piece, corner ^ mask, 0)
    slab = slab.reshape(4 * j_rows, quarter)
    whole_in = outer_gather(own_in, outer, place).transpose(1, 0, 2, 3).reshape(2, quarter, width)
    whole_out = outer_gather(slab, outer, place).reshape(outer * 4 * j_rows, quarter)

    base_part = jnp.sum(jnp.square(whole_out.astype(jnp.float32)), axis=-1)
    base_part = base_part + pair_swap(base_part, 1)
    base_sum = base_part + pair_swap(base_part, 2)

    gate_pre = jnp.einsum("td,fd->tf", all_keys, whole_in[0], preferred_element_type=jnp.float32)
    up_pre = jnp.einsum("td,fd->tf", all_keys, whole_in[1], preferred_element_type=jnp.float32)
    d_act = jnp.dot(all_target, whole_out, preferred_element_type=jnp.float32)
    sigmoid_h = jax.nn.sigmoid(gate_pre)
    silu_gate = gate_pre * sigmoid_h
    activation = (silu_gate * up_pre).astype(jnp.bfloat16)
    d_gate = (d_act * up_pre * (sigmoid_h * (1.0 + gate_pre * (1.0 - sigmoid_h)))).astype(jnp.bfloat16)
    d_up = (d_act * silu_gate).astype(jnp.bfloat16)
    g_gate = jnp.einsum("tf,td->fd", d_gate, all_keys, preferred_element_type=jnp.float32)
    g_up = jnp.einsum("tf,td->fd", d_up, all_keys, preferred_element_type=jnp.float32)
    g_out = jnp.einsum("tj,tf->jf", all_target, activation, preferred_element_type=jnp.float32)

    g_in = jnp.stack([g_gate.reshape(outer, f_rows, width), g_up.reshape(outer, f_rows, width)], 1)
    grad_in = outer_sum(g_in, outer, place)
    grad_out = outer_sum(g_out.reshape(outer, 4 * j_rows, quarter), outer, place)

    base = own_in.astype(jnp.float32)
    moved = base + grad_in
    base_rms = jnp.sqrt(jnp.mean(base * base, axis=-1, keepdims=True) + EPS)
    moved_rms = jnp.sqrt(jnp.mean(moved * moved, axis=-1, keepdims=True) + EPS)
    new_in = (moved * (base_rms / moved_rms)).astype(jnp.bfloat16)
    moved_out = (slab.astype(jnp.float32) + grad_out).astype(jnp.bfloat16)

    fast_in = outer_gather(new_in, outer, place).transpose(1, 0, 2, 3).reshape(2, quarter, width)
    fast_out = outer_gather(moved_out, outer, place).reshape(outer * 4 * j_rows, quarter)
    for mask in (2, 1):
        fast_in = jnp.concatenate([fast_in, pair_swap(fast_in, mask)], 1)
        fast_out = jnp.concatenate([fast_out, pair_swap(fast_out, mask)], 1)
    units = fast_out.shape[1]
    moved_sum = jnp.sum(jnp.square(fast_out.astype(jnp.float32)), axis=-1)
    out_scale = (jnp.sqrt(base_sum / units + EPS) / jnp.sqrt(moved_sum / units + EPS))[None, :]

    depth = lax.axis_size("segment")
    first = lax.axis_index("segment") == 0
    finished = apply_layer(inputs, gains[0], fast_in[0], fast_in[1], fast_out, out_scale)
    for _ in range(depth - 1):
        arrived = lax.ppermute(finished, "segment", [(i, i + 1) for i in range(depth - 1)])
        current = jnp.where(first, inputs, arrived)
        finished = apply_layer(current, gains[0], fast_in[0], fast_in[1], fast_out, out_scale)
    return finished[None]


def per_device(inputs, keys, values, rates, gains, w_in, w_out):
    rows_fit = w_in.shape[1] % 8 == 0 and w_out.shape[1] % 16 == 0 and inputs.shape[0] % LANES == 0
    part = 4 * w_out.shape[1] % LANES
    fits = rows_fit and (part == 0 or LANES % part == 0)
    device = fast_device if fits else plain_device
    return device(inputs, keys, values, rates, gains, w_in, w_out)


def solution(mesh):
    in_specs = (
        P("tok", None),
        P("segment", "tok", None),
        P("segment", "tok", None),
        P("segment", "tok"),
        P("segment", None),
        P("segment", "tok", None, None),
        P("segment", "tok", None),
    )
    out_specs = P("segment", "tok", None)
    return jax.shard_map(
        per_device, mesh=mesh, in_specs=in_specs, out_specs=out_specs, check_vma=False
    )
```

```python
import functools

import jax
import jax.numpy as jnp
import numpy as np
from jax import lax
from jax.experimental import pallas as pl
from jax.experimental.pallas import tpu as pltpu
from jax.sharding import PartitionSpec as P

EPS = 1e-06
LANES = 128
GRANT = 12 * 2**20
F32, BF16 = jnp.float32, jnp.bfloat16


def tok_shift(block, route):
    count = lax.axis_size("tok")
    return lax.ppermute(block, "tok", [(i, route(i)) for i in range(count)])


def pair_swap(block, mask):
    return tok_shift(block, lambda i: i ^ mask)


def outer_shift(block, distance, outer):
    return tok_shift(block, lambda i: ((i // 4 + distance) % outer) * 4 + i % 4)


def call(body, name, outs, *args, scratch=(), flops=0):
    moved = sum(a.size * a.dtype.itemsize for a in args) + sum(o.size * o.dtype.itemsize for o in outs)
    return pl.pallas_call(
        body,
        name=name,
        out_shape=tuple(outs),
        in_specs=[pl.BlockSpec(memory_space=pltpu.VMEM)] * len(args),
        out_specs=tuple(pl.BlockSpec(memory_space=pltpu.VMEM) for _ in outs),
        scratch_shapes=list(scratch),
        compiler_params=pltpu.CompilerParams(vmem_limit_bytes=GRANT),
        cost_estimate=pl.CostEstimate(flops=flops, bytes_accessed=moved, transcendentals=0),
    )(*args)


def like(shape, dtype=BF16):
    return jax.ShapeDtypeStruct(shape, dtype)


def dot_nt(a, b):
    return lax.dot_general(a, b, (((1,), (1,)), ((), ())), preferred_element_type=F32)


def dot_nn(a, b):
    return lax.dot_general(a, b, (((1,), (0,)), ((), ())), preferred_element_type=F32)


def pack(block):
    rows, cols = block.shape
    whole = cols // LANES * LANES
    parts = [block[:, i : i + LANES] for i in range(0, whole, LANES)]
    if cols > whole:
        ways = LANES // (cols - whole)
        step = rows // ways
        parts.append(jnp.concatenate([block[i * step : (i + 1) * step, whole:] for i in range(ways)], 1))
    return jnp.concatenate(parts, 0)


def unpack(packed, rows, cols):
    whole = cols // LANES * LANES
    parts = [packed[i * rows : (i + 1) * rows] for i in range(whole // LANES)]
    if cols > whole:
        rest = cols - whole
        tail = packed[whole // LANES * rows :]
        parts.append(jnp.concatenate([tail[:, i : i + rest] for i in range(0, LANES, rest)], 0))
    return jnp.concatenate(parts, 1)


def prepare_body(values, rates, w_in, w_out, order, target, own_in, *rest):
    pieces, by_corner = rest[:4], rest[4]
    corner = lax.axis_index("tok") % 4
    wide = jnp.broadcast_to(rates[...], (8, rates.shape[1]))
    column = wide.T[:, 0:1]
    target[...] = (column * values[...].astype(F32)).astype(BF16)
    pair = w_in[...].astype(F32)
    own_in[0] = pair[:, 0, :].astype(BF16)
    own_in[1] = pair[:, 1, :].astype(BF16)
    sorted_out = dot_nn(w_out[...], order[...])
    quarter = by_corner.shape[2]
    for c in range(4):
        by_corner[c] = sorted_out[:, c * quarter : (c + 1) * quarter]
    for mask in range(4):
        pieces[mask][...] = by_corner[corner ^ mask].astype(BF16)


def slab_body(*refs):
    pieces, slab, rows = refs[:4], refs[4], refs[5]
    corner = lax.axis_index("tok") % 4
    for mask in range(4):
        rows[corner ^ mask] = pieces[mask][...].astype(F32)
    block = rows[...]
    slab[...] = pack(block.reshape(block.shape[0] * block.shape[1], block.shape[2]).T).astype(BF16)


def place_in(pieces, out, outer):
    place = lax.axis_index("tok") // 4
    for k in range(outer):
        home = lax.rem(place + outer - k, outer)
        out[0, home] = pieces[k][0]
        out[1, home] = pieces[k][1]


def place_out(pieces, spread, outer, rows, cols):
    place = lax.axis_index("tok") // 4
    for k in range(outer):
        spread[lax.rem(place + outer - k, outer)] = pieces[k][...].astype(F32)
    return jnp.concatenate([unpack(spread[z], rows, cols) for z in range(outer)], 1)


def grads(keys, target, w_gate, w_up, w_down):
    gate_pre, up_pre = dot_nt(w_gate, keys), dot_nt(w_up, keys)
    d_act = dot_nt(w_down, target)
    sigmoid_h = jax.nn.sigmoid(gate_pre)
    silu_gate = gate_pre * sigmoid_h
    activation = (silu_gate * up_pre).astype(BF16)
    d_gate = (d_act * up_pre * (sigmoid_h * (1.0 + gate_pre * (1.0 - sigmoid_h)))).astype(BF16)
    d_up = (d_act * silu_gate).astype(BF16)
    return dot_nn(d_gate, keys), dot_nn(d_up, keys), dot_nn(activation, target)


def rows_of(ref, index):
    block = ref[index].astype(F32)
    return block.reshape(block.shape[0] * block.shape[1], block.shape[2]).astype(BF16)


def near_body(outer, cols, *refs):
    in_pieces, out_pieces = refs[:outer], refs[outer : 2 * outer]
    keys_a, keys_b, target_a, target_b = refs[2 * outer : 2 * outer + 4]
    whole_in, whole_out, base_part, acc_gate, acc_up, acc_out = refs[2 * outer + 4 : 2 * outer + 10]
    spread = refs[2 * outer + 10]
    place_in(in_pieces, whole_in, outer)
    w_down = place_out(out_pieces, spread, outer, acc_gate.shape[0], cols)
    base_part[...] = jnp.sum(w_down * w_down, axis=0, keepdims=True)
    w_down = w_down.astype(BF16)
    whole_out[...] = w_down
    w_gate, w_up = rows_of(whole_in, 0), rows_of(whole_in, 1)
    first = grads(keys_a[...], target_a[...], w_gate, w_up, w_down)
    second = grads(keys_b[...], target_b[...], w_gate, w_up, w_down)
    for ref, a, b in zip((acc_gate, acc_up, acc_out), first, second):
        ref[...] = a + b


def far_body(outer, cols, *refs):
    whole_in, whole_out, keys_a, keys_b, target_a, target_b, acc_gate, acc_up, acc_out = refs[:9]
    in_sent, out_sent = refs[9 : 9 + outer], refs[9 + outer : 9 + 2 * outer]
    spread_gate, spread_up, spread_out = refs[9 + 2 * outer :]
    place = lax.axis_index("tok") // 4
    w_gate, w_up, w_down = rows_of(whole_in, 0), rows_of(whole_in, 1), whole_out[...]
    first = grads(keys_a[...], target_a[...], w_gate, w_up, w_down)
    second = grads(keys_b[...], target_b[...], w_gate, w_up, w_down)
    total = [ref[...] + a + b for ref, a, b in zip((acc_gate, acc_up, acc_out), first, second)]
    spread_gate[...] = total[0].reshape(spread_gate.shape)
    spread_up[...] = total[1].reshape(spread_up.shape)
    for z in range(outer):
        spread_out[z] = pack(total[2][:, z * cols : (z + 1) * cols])
    for k in range(outer):
        home = lax.rem(place + k, outer)
        in_sent[k][0] = spread_gate[home].astype(in_sent[k].dtype)
        in_sent[k][1] = spread_up[home].astype(in_sent[k].dtype)
        out_sent[k][...] = spread_out[home].astype(out_sent[k].dtype)


def join_in_body(outer, *refs):
    place_in(refs[:outer], refs[outer], outer)


def join_out_body(outer, cols, *refs):
    whole, spread = refs[outer], refs[outer + 1]
    whole[...] = place_out(refs[:outer], spread, outer, whole.shape[0], cols).astype(BF16)


def layer_body(rows_a, rows_b, gain, base_sum, *refs):
    in_parts, out_parts, result = refs[:4], refs[4:8], refs[8]
    rows = jnp.where(lax.axis_index("segment") == 0, rows_a[...], rows_b[...])
    rows32 = rows.astype(F32)
    scale = lax.rsqrt(jnp.mean(rows32 * rows32, axis=-1, keepdims=True) + EPS)
    normed = (rows32 * scale * gain[...]).astype(BF16)
    w_gate = jnp.concatenate([part[0] for part in in_parts], 0)
    w_up = jnp.concatenate([part[1] for part in in_parts], 0)
    w_down = jnp.concatenate([part[...] for part in out_parts], 0)
    units = w_down.shape[0]
    wide = w_down.astype(F32)
    moved_sum = jnp.sum(wide * wide, axis=0, keepdims=True)
    out_scale = jnp.sqrt(base_sum[...] / units + EPS) / jnp.sqrt(moved_sum / units + EPS)
    gate_pre, up_pre = dot_nt(normed, w_gate), dot_nt(normed, w_up)
    mixed = (gate_pre * jax.nn.sigmoid(gate_pre) * up_pre).astype(BF16)
    result[...] = (rows32 + dot_nn(mixed, w_down) * out_scale).astype(BF16)


def column_order(outer, f_rows):
    units = outer * 4 * f_rows
    source = np.arange(units).reshape(outer, 4, f_rows).transpose(1, 0, 2).reshape(-1)
    order = np.zeros((units, units), np.float32)
    order[source, np.arange(units)] = 1.0
    return jnp.asarray(order, BF16)


def fast_device(inputs, keys, values, rates, gains, w_in, w_out):
    own_keys = keys[0]
    tokens, width = own_keys.shape
    outer = lax.axis_size("tok") // 4
    f_rows, j_rows = w_in.shape[1], w_out.shape[1]
    quarter, cols = outer * f_rows, 4 * j_rows
    packed = (quarter * cols // LANES, LANES)

    y_keys = pair_swap(own_keys, 2)
    made = call(
        prepare_body,
        "prepare",
        [like((tokens, width)), like((2, f_rows, width))] + [like((j_rows, quarter))] * 4,
        values[0], rates, w_in[0], w_out[0], column_order(outer, f_rows),
        scratch=[pltpu.VMEM((4, j_rows, quarter), F32)],
    )
    own_target, own_in, pieces = made[0], made[1], made[2:]
    pieces = [pieces[0]] + [pair_swap(pieces[mask], mask) for mask in (1, 2, 3)]
    (slab,) = call(
        slab_body, "slab", [like(packed)], *pieces, scratch=[pltpu.VMEM((4, j_rows, quarter), F32)]
    )
    in_pieces = [own_in] + [outer_shift(own_in, k, outer) for k in range(1, outer)]
    y_target = pair_swap(own_target, 2)
    core_keys, core_target = pair_swap(own_keys, 1), pair_swap(own_target, 1)
    far_keys, far_target = pair_swap(y_keys, 1), pair_swap(y_target, 1)
    out_pieces = [slab] + [outer_shift(slab, k, outer) for k in range(1, outer)]

    spread = pltpu.VMEM((outer,) + packed, F32)
    work = 2 * 2 * 6 * tokens * width * quarter
    whole_in, whole_out, base_part, acc_gate, acc_up, acc_out = call(
        functools.partial(near_body, outer, cols),
        "near",
        [like((2, outer, f_rows, width)), like((quarter, width)), like((1, width), F32)]
        + [like((quarter, width), F32)] * 3,
        *in_pieces, *out_pieces, own_keys, core_keys, own_target, core_target,
        scratch=[spread],
        flops=work,
    )
    base_part = base_part + pair_swap(base_part, 1)
    base_sum = base_part + pair_swap(base_part, 2)
    made = call(
        functools.partial(far_body, outer, cols),
        "far",
        [like((2, f_rows, width), BF16 if k else F32) for k in range(outer)]
        + [like(packed, BF16 if k else F32) for k in range(outer)],
        whole_in, whole_out, y_keys, far_keys, y_target, far_target, acc_gate, acc_up, acc_out,
        scratch=[pltpu.VMEM((outer, f_rows, width), F32)] * 2 + [spread],
        flops=work,
    )
    grad_in, grad_out = made[0], made[outer]
    for k in range(1, outer):
        grad_in = grad_in + outer_shift(made[k], k, outer).astype(F32)
    for k in range(1, outer):
        grad_out = grad_out + outer_shift(made[outer + k], k, outer).astype(F32)

    base = own_in.astype(F32)
    moved = base + grad_in
    base_rms = jnp.sqrt(jnp.mean(base * base, axis=-1, keepdims=True) + EPS)
    moved_rms = jnp.sqrt(jnp.mean(moved * moved, axis=-1, keepdims=True) + EPS)
    new_in = (moved * (base_rms / moved_rms)).astype(BF16)
    moved_out = (slab.astype(F32) + grad_out).astype(BF16)

    (fast_in,) = call(
        functools.partial(join_in_body, outer),
        "join_in",
        [like((2, outer, f_rows, width))],
        new_in, *[outer_shift(new_in, k, outer) for k in range(1, outer)],
    )
    fast_in = fast_in.reshape(2, quarter, width)
    (fast_out,) = call(
        functools.partial(join_out_body, outer, cols),
        "join_out",
        [like((quarter, width))],
        moved_out, *[outer_shift(moved_out, k, outer) for k in range(1, outer)],
        scratch=[spread],
    )
    weights = []
    for own in (fast_in, fast_out):
        other = pair_swap(own, 2)
        weights += [own, other, pair_swap(own, 1), pair_swap(other, 1)]

    def apply_layer(arrived):
        (rows,) = call(
            layer_body, "layer", [like(inputs.shape)], inputs, arrived, gains, base_sum, *weights,
            flops=6 * tokens * width * 4 * quarter,
        )
        return rows

    depth = lax.axis_size("segment")
    finished = apply_layer(inputs)
    for _ in range(depth - 1):
        finished = apply_layer(lax.ppermute(finished, "segment", [(i, i + 1) for i in range(depth - 1)]))
    return finished[None]


def outer_gather(block, outer, place):
    pieces = jnp.zeros((outer,) + block.shape, block.dtype)
    for distance in range(outer):
        piece = outer_shift(block, distance, outer) if distance else block
        pieces = lax.dynamic_update_index_in_dim(pieces, piece, (place - distance) % outer, 0)
    return pieces


def outer_sum(pieces, outer, place):
    total = lax.dynamic_index_in_dim(pieces, place, 0, keepdims=False)
    for distance in range(1, outer):
        sent = lax.dynamic_index_in_dim(pieces, (place + distance) % outer, 0, keepdims=False)
        total = total + outer_shift(sent.astype(jnp.bfloat16), distance, outer).astype(jnp.float32)
    return total


def apply_layer(rows_in, gain_row, fast_gate, fast_up, fast_out, out_scale):
    rows32 = rows_in.astype(jnp.float32)
    scale = lax.rsqrt(jnp.mean(rows32 * rows32, axis=-1, keepdims=True) + EPS)
    normed = (rows32 * scale * gain_row).astype(jnp.bfloat16)
    gate_pre = jnp.einsum("td,fd->tf", normed, fast_gate, preferred_element_type=jnp.float32)
    up_pre = jnp.einsum("td,fd->tf", normed, fast_up, preferred_element_type=jnp.float32)
    mixed = (gate_pre * jax.nn.sigmoid(gate_pre) * up_pre).astype(jnp.bfloat16)
    branch = jnp.einsum("tf,jf->tj", mixed, fast_out, preferred_element_type=jnp.float32)
    return (rows32 + branch * out_scale).astype(jnp.bfloat16)


def plain_device(inputs, keys, values, rates, gains, w_in, w_out):
    own_keys = keys[0]
    own_target = (rates[0][:, None] * values[0].astype(jnp.float32)).astype(jnp.bfloat16)
    width = own_keys.shape[1]
    outer = lax.axis_size("tok") // 4
    index = lax.axis_index("tok")
    place, corner = index // 4, index % 4
    f_rows, j_rows = w_in.shape[1], w_out.shape[1]
    quarter = outer * f_rows

    y_keys, y_target = pair_swap(own_keys, 2), pair_swap(own_target, 2)
    all_keys = jnp.concatenate([own_keys, pair_swap(own_keys, 1), y_keys, pair_swap(y_keys, 1)], 0)
    all_target = jnp.concatenate([own_target, pair_swap(own_target, 1), y_target, pair_swap(y_target, 1)], 0)

    own_in = w_in[0].transpose(1, 0, 2)
    by_corner = w_out[0].reshape(j_rows, outer, 4, f_rows).transpose(2, 0, 1, 3).reshape(4, j_rows, quarter)
    slab = jnp.zeros((4, j_rows, quarter), jnp.bfloat16)
    for mask in range(4):
        piece = lax.dynamic_index_in_dim(by_corner, corner ^ mask, 0, keepdims=False)
        piece = pair_swap(piece, mask) if mask else piece
        slab = lax.dynamic_update_index_in_dim(slab, piece, corner ^ mask, 0)
    slab = slab.reshape(4 * j_rows, quarter)
    whole_in = outer_gather(own_in, outer, place).transpose(1, 0, 2, 3).reshape(2, quarter, width)
    whole_out = outer_gather(slab, outer, place).reshape(outer * 4 * j_rows, quarter)

    base_part = jnp.sum(jnp.square(whole_out.astype(jnp.float32)), axis=-1)
    base_part = base_part + pair_swap(base_part, 1)
    base_sum = base_part + pair_swap(base_part, 2)

    gate_pre = jnp.einsum("td,fd->tf", all_keys, whole_in[0], preferred_element_type=jnp.float32)
    up_pre = jnp.einsum("td,fd->tf", all_keys, whole_in[1], preferred_element_type=jnp.float32)
    d_act = jnp.dot(all_target, whole_out, preferred_element_type=jnp.float32)
    sigmoid_h = jax.nn.sigmoid(gate_pre)
    silu_gate = gate_pre * sigmoid_h
    activation = (silu_gate * up_pre).astype(jnp.bfloat16)
    d_gate = (d_act * up_pre * (sigmoid_h * (1.0 + gate_pre * (1.0 - sigmoid_h)))).astype(jnp.bfloat16)
    d_up = (d_act * silu_gate).astype(jnp.bfloat16)
    g_gate = jnp.einsum("tf,td->fd", d_gate, all_keys, preferred_element_type=jnp.float32)
    g_up = jnp.einsum("tf,td->fd", d_up, all_keys, preferred_element_type=jnp.float32)
    g_out = jnp.einsum("tj,tf->jf", all_target, activation, preferred_element_type=jnp.float32)

    g_in = jnp.stack([g_gate.reshape(outer, f_rows, width), g_up.reshape(outer, f_rows, width)], 1)
    grad_in = outer_sum(g_in, outer, place)
    grad_out = outer_sum(g_out.reshape(outer, 4 * j_rows, quarter), outer, place)

    base = own_in.astype(jnp.float32)
    moved = base + grad_in
    base_rms = jnp.sqrt(jnp.mean(base * base, axis=-1, keepdims=True) + EPS)
    moved_rms = jnp.sqrt(jnp.mean(moved * moved, axis=-1, keepdims=True) + EPS)
    new_in = (moved * (base_rms / moved_rms)).astype(jnp.bfloat16)
    moved_out = (slab.astype(jnp.float32) + grad_out).astype(jnp.bfloat16)

    fast_in = outer_gather(new_in, outer, place).transpose(1, 0, 2, 3).reshape(2, quarter, width)
    fast_out = outer_gather(moved_out, outer, place).reshape(outer * 4 * j_rows, quarter)
    for mask in (2, 1):
        fast_in = jnp.concatenate([fast_in, pair_swap(fast_in, mask)], 1)
        fast_out = jnp.concatenate([fast_out, pair_swap(fast_out, mask)], 1)
    units = fast_out.shape[1]
    moved_sum = jnp.sum(jnp.square(fast_out.astype(jnp.float32)), axis=-1)
    out_scale = (jnp.sqrt(base_sum / units + EPS) / jnp.sqrt(moved_sum / units + EPS))[None, :]

    depth = lax.axis_size("segment")
    first = lax.axis_index("segment") == 0
    finished = apply_layer(inputs, gains[0], fast_in[0], fast_in[1], fast_out, out_scale)
    for _ in range(depth - 1):
        arrived = lax.ppermute(finished, "segment", [(i, i + 1) for i in range(depth - 1)])
        current = jnp.where(first, inputs, arrived)
        finished = apply_layer(current, gains[0], fast_in[0], fast_in[1], fast_out, out_scale)
    return finished[None]


def per_device(inputs, keys, values, rates, gains, w_in, w_out):
    rows_fit = w_in.shape[1] % 8 == 0 and w_out.shape[1] % 16 == 0 and inputs.shape[0] % LANES == 0
    part = 4 * w_out.shape[1] % LANES
    fits = rows_fit and (part == 0 or LANES % part == 0)
    device = fast_device if fits else plain_device
    return device(inputs, keys, values, rates, gains, w_in, w_out)


def solution(mesh):
    in_specs = (
        P("tok", None),
        P("segment", "tok", None),
        P("segment", "tok", None),
        P("segment", "tok"),
        P("segment", None),
        P("segment", "tok", None, None),
        P("segment", "tok", None),
    )
    out_specs = P("segment", "tok", None)
    return jax.shard_map(
        per_device, mesh=mesh, in_specs=in_specs, out_specs=out_specs, check_vma=False
    )
```
